512 devices in a mesh: mesh: 64 (over z_hi, y, x, core), col: 8 (over z_lo).
Axes of the slice: x: 4, y: 4, z: 16 (z_hi: 2, z_lo: 8; z = z_hi * 8 + z_lo), core: 2. Of those that a mesh axis runs over, the one named last changes fastest.
Arguments:
- basis: bfloat16 [786432, 512], P(('mesh', 'col')), may hold values from -24 to 24
- jac_blocks: bfloat16 [12288, 8, 64, 64], P(('mesh', 'col')), may hold values from -0.25 to 0.25
- block_cols: int32 [12288, 8], P(('mesh', 'col')), may hold values from 0 to 12287, as said below
- live_slots: int32 [12288], P(('mesh', 'col')), may hold values from 1 to 8
- accumulation: float32 [786432], P(('mesh', 'col')), may hold values from 0.5 to 4
Outputs:
- image: bfloat16 [786432, 512], P(('mesh', 'col'))
- projected: float32 [512, 512], P('mesh', 'col')
The draws below stay inside these ranges and needn't reach their ends.
Inputs may be any that keep to these rules, and one draw needn't show every extreme that they name: `block_cols`: each block row's column blocks lie within 2 block rows of it, and some lie exactly 2 away on either side.
All inputs are finite; a program needn't handle non-finite values.
Results may differ from the reference program's by a relative error of at most 0.003.
Values may be sent and summed in bfloat16 or wider, within the bound.
A program may use at most 64 MiB of HBM per device.

```python
import math
import jax
import jax.numpy as jnp
from jax import lax

BS = 64
K = 512
SLOTS = 8
REACH = 2
RD = 24
NBLOCKS = 12288
NROWS = 786432


def draw_block_cols(key, part):
    offsets = jax.random.randint(key, (NBLOCKS, SLOTS), -REACH, REACH + 1)
    rowids = jnp.arange(NBLOCKS, dtype=jnp.int32)[:, None]
    return jnp.clip(rowids + offsets, 0, NBLOCKS - 1).astype(jnp.int32)


def touch_ends(array, own_key, smallest, largest):
    place = [jax.random.randint(jax.random.fold_in(own_key, axis), (), 0, length) for axis, length in enumerate(array.shape)]
    main_axis = array.shape.index(max(array.shape))
    neighbour = place[:main_axis] + [(place[main_axis] + 1) % array.shape[main_axis]] + place[main_axis + 1:]
    return array.at[tuple(place)].set(smallest).at[tuple(neighbour)].set(largest)


def raised(values, own_key, source, target, blocks, factor):
    def block_of(dim):
        return (jnp.arange(values.shape[dim]) // (values.shape[dim] // blocks)).reshape((-1,) + (1,) * (values.ndim - 1 - dim))

    first = jax.random.permutation(own_key, blocks)[block_of(target)]
    far = (block_of(target) + blocks // 2) % blocks
    return jnp.where((block_of(source) == first) | (block_of(source) == far), factor * values, values)


def shard_levels(key, extent, shards, least, high):
    loudness, own = 1.0, jax.random.fold_in(key, 6)
    for axis_at, shards_of in shards:
        heights = jnp.exp(jax.random.uniform(jax.random.fold_in(own, axis_at), (shards_of,), jnp.float32, least / len(shards), high / len(shards)))
        loudness = loudness * jnp.repeat(heights, extent[axis_at] // shards_of).reshape([-1 if axis == axis_at else 1 for axis in range(len(extent))])
    return loudness


def normal_values(rng, dims, scale, limit, shards=(), kind=jnp.bfloat16):
    gain = shard_levels(rng, dims, shards, -0.22, 0.18) if shards else 1.0
    values = jax.random.normal(rng, dims, jnp.float32) * scale * gain
    return jnp.minimum(jnp.maximum(values, -limit), limit).astype(kind)


def heavy_noise(key, shape, scale, bound, cuts, heavy, kind=jnp.bfloat16):
    result = scale * jax.random.normal(key, shape, jnp.float32)
    if cuts:
        result = result * shard_levels(key, shape, cuts, -0.22, 0.18)
    return jnp.clip(raised(result, jax.random.fold_in(key, 3), *heavy), -bound, bound).astype(kind)


def setup_inputs(seed: int = 0) -> dict:
    key_list = jax.random.split(jax.random.key(seed), 6)
    return {
        "basis": heavy_noise(key_list[0], (NROWS, K), 1.0, 24.0, ((0, 512),), (0, 1, 512, 6.0)),
        "jac_blocks": normal_values(key_list[1], (NBLOCKS, SLOTS, BS, BS), (BS * SLOTS) ** -0.5, 0.25, ((0, 512),)),
        "block_cols": draw_block_cols(jax.random.fold_in(key_list[5], 71), 0),
        "live_slots": touch_ends(jax.random.randint(key_list[3], (NBLOCKS,), 1, SLOTS + 1), jax.random.fold_in(key_list[3], 1), 1, SLOTS).astype(jnp.int32),
        "accumulation": jnp.clip(jnp.exp(math.log(4.0) - 2.0794415 * jax.random.uniform(key_list[4], (NROWS,), jnp.float32) ** shard_levels(key_list[4], (NROWS,), ((0, 512),), -0.2, 0.2)), 0.5, 4.0),
    }


def reference(basis, jac_blocks, block_cols, live_slots, accumulation):
    nblk = jac_blocks.shape[0]
    width = basis.shape[1]
    vblocks = basis.reshape(nblk, BS, width)
    groups = nblk // RD

    def one_group(args):
        jac, cols, live = args
        picked = vblocks[cols].astype(jnp.float32)
        keep = (jnp.arange(SLOTS, dtype=jnp.int32)[None, :] < live[:, None]).astype(jnp.float32)
        masked = jac.astype(jnp.float32) * keep[:, :, None, None]
        return jnp.einsum('rsab,rsbk->rak', masked, picked)

    coupled = lax.map(one_group, (jac_blocks.reshape(groups, RD, SLOTS, BS, BS), block_cols.reshape(groups, RD, SLOTS), live_slots.reshape(groups, RD)))
    coupled = coupled.reshape(nblk * BS, width)
    image = (coupled + accumulation[:, None] * basis.astype(jnp.float32)).astype(jnp.bfloat16)
    projected = jnp.dot(basis.T, image, preferred_element_type=jnp.float32) * (1.0 / NROWS)
    return image, projected
```

```python
import functools

import jax
import jax.numpy as jnp
from jax import lax
from jax.experimental import pallas as pl
from jax.experimental.pallas import tpu as pltpu
from jax.sharding import PartitionSpec as P

REACH = 2
MESH = pl.DeviceIdType.MESH
NCORE, NX, NY, NZH = 2, 4, 4, 2


def with_halo(block, sides, width):
    for axis, dim in sides:
        count = lax.axis_size(axis)
        forward = [(i, i + 1) for i in range(count - 1)]
        backward = [(target, source) for source, target in forward]
        low = lax.ppermute(
            lax.slice_in_dim(block, block.shape[dim] - width, None, axis=dim), axis, forward
        )
        high = lax.ppermute(lax.slice_in_dim(block, 0, width, axis=dim), axis, backward)
        block = jnp.concatenate([low, block, high], axis=dim)
    return block


def scatter_kernel(scale, p_ref, o_ref, pair_in, plane_out, plane_in, line_out, line_in, sems0, s1, r1, s2, r2):
    m = lax.axis_index("mesh")
    c = lax.axis_index("col")
    core = m % NCORE
    x = (m // NCORE) % NX
    y = (m // (NCORE * NX)) % NY
    zh = m // (NCORE * NX * NY)
    ncol = line_out.shape[0] // NZH
    nplane, nline = NX * NY, NZH * ncol
    rows = p_ref.shape[2] // NZH
    wide = p_ref.shape[3] // ncol
    z = zh * ncol + c

    def plane_peer(k):
        px = (x + k % NX) % NX
        py = (y + k // NX) % NY
        return py * NX + px, (((zh * NY + py) * NX + px) * NCORE + core, c)

    def line_peer(k):
        pz = (z + k) % nline
        return pz, ((pz // ncol) * (NCORE * NX * NY) + m % (NCORE * NX * NY), pz % ncol)

    pair = (m + 1 - 2 * core, c)

    barrier = pltpu.get_barrier_semaphore()
    pl.semaphore_signal(barrier, inc=1, device_id=pair, device_id_type=MESH)
    for k in range(1, nplane):
        pl.semaphore_signal(barrier, inc=1, device_id=plane_peer(k)[1], device_id_type=MESH)
    for k in range(1, nline):
        pl.semaphore_signal(barrier, inc=1, device_id=line_peer(k)[1], device_id_type=MESH)
    pl.semaphore_wait(barrier, 1 + (nplane - 1) + (nline - 1))

    copy0 = pltpu.make_async_remote_copy(
        src_ref=p_ref.at[1 - core], dst_ref=pair_in, send_sem=sems0.at[0], recv_sem=sems0.at[1],
        device_id=pair, device_id_type=MESH,
    )
    copy0.start()
    copy0.wait()

    copies1 = []
    for k in range(1, nplane):
        j, dev = plane_peer(k)
        plane_out[j] = (p_ref[core, j].astype(jnp.float32) + pair_in[j].astype(jnp.float32)).astype(plane_out.dtype)
        copy = pltpu.make_async_remote_copy(
            src_ref=plane_out.at[j], dst_ref=plane_in.at[k - 1], send_sem=s1.at[k - 1], recv_sem=r1.at[k - 1],
            device_id=dev, device_id_type=MESH,
        )
        copy.start()
        copies1.append(copy)
    own = y * NX + x
    acc = p_ref[core, own].astype(jnp.float32) + pair_in[own].astype(jnp.float32)
    for k in range(1, nplane):
        copies1[k - 1].wait_recv()
        acc += plane_in[k - 1].astype(jnp.float32)

    for h in range(NZH):
        for q in range(ncol):
            line_out[h * ncol + q] = acc[h * rows:(h + 1) * rows, q * wide:(q + 1) * wide]
    copies2 = []
    for k in range(1, nline):
        j, dev = line_peer(k)
        copy = pltpu.make_async_remote_copy(
            src_ref=line_out.at[j], dst_ref=line_in.at[k - 1], send_sem=s2.at[k - 1], recv_sem=r2.at[k - 1],
            device_id=dev, device_id_type=MESH,
        )
        copy.start()
        copies2.append(copy)
    total = line_out[z]
    for k in range(1, nline):
        copies2[k - 1].wait_recv()
        total += line_in[k - 1]
    o_ref[...] = total * scale
    for copy in copies1 + copies2:
        copy.wait_send()


def scatter_sum(partial, scale):
    mesh_count, ncol = lax.axis_size("mesh"), lax.axis_size("col")
    nrow, ncols = partial.shape
    rows, wide = nrow // mesh_count, ncols // ncol
    nplane, nline = NX * NY, NZH * ncol
    p = partial.reshape(NZH, NY, NX, NCORE, rows, ncols).transpose(3, 1, 2, 0, 4, 5)
    p = p.reshape(NCORE, nplane, NZH * rows, ncols).astype(jnp.bfloat16)
    return pl.pallas_call(
        functools.partial(scatter_kernel, scale),
        out_shape=jax.ShapeDtypeStruct((rows, wide), jnp.float32),
        in_specs=[pl.BlockSpec(memory_space=pltpu.VMEM)],
        out_specs=pl.BlockSpec(memory_space=pltpu.VMEM),
        scratch_shapes=[
            pltpu.VMEM((nplane, NZH * rows, ncols), jnp.bfloat16),
            pltpu.VMEM((nplane, NZH * rows, ncols), jnp.bfloat16),
            pltpu.VMEM((nplane - 1, NZH * rows, ncols), jnp.bfloat16),
            pltpu.VMEM((nline, rows, wide), jnp.float32),
            pltpu.VMEM((nline - 1, rows, wide), jnp.float32),
            pltpu.SemaphoreType.DMA((2,)),
            pltpu.SemaphoreType.DMA((nplane - 1,)),
            pltpu.SemaphoreType.DMA((nplane - 1,)),
            pltpu.SemaphoreType.DMA((nline - 1,)),
            pltpu.SemaphoreType.DMA((nline - 1,)),
        ],
        compiler_params=pltpu.CompilerParams(collective_id=0, has_side_effects=True),
    )(p)


def local(basis, jac_blocks, block_cols, live_slots, accumulation):
    nrows, width = basis.shape
    nblk, slots, bsize, _ = jac_blocks.shape
    padded = with_halo(basis, ((("mesh", "col"), 0),), REACH * bsize)
    first = lax.axis_index(("mesh", "col")) * nblk
    local_cols = block_cols - first + REACH
    pblocks = padded.reshape(nblk + 2 * REACH, bsize, width)
    picked = pblocks[local_cols]
    keep = lax.broadcasted_iota(jnp.int32, (nblk, slots), 1) < live_slots[:, None]
    masked = jnp.where(keep[:, :, None, None], jac_blocks, jnp.zeros_like(jac_blocks))
    coupled = jnp.einsum("rsab,rsbk->rak", masked, picked, preferred_element_type=jnp.float32)
    coupled = coupled.reshape(nrows, width)
    image = (coupled + accumulation[:, None] * basis.astype(jnp.float32)).astype(jnp.bfloat16)
    total_rows = nrows * lax.axis_size("mesh") * lax.axis_size("col")
    dims = (((0,), (0,)), ((), ()))
    partial = lax.dot_general(basis, image, dims, preferred_element_type=jnp.float32)
    projected = scatter_sum(partial, 1.0 / total_rows)
    return (image, projected)


def solution(mesh):
    return jax.shard_map(
        local,
        mesh=mesh,
        in_specs=(
            P(("mesh", "col"), None),
            P(("mesh", "col"), None, None, None),
            P(("mesh", "col"), None),
            P(("mesh", "col")),
            P(("mesh", "col")),
        ),
        out_specs=(P(("mesh", "col"), None), P("mesh", "col")),
        check_vma=False,
    )
```

```python
import functools

import jax
import jax.numpy as jnp
from jax import lax
from jax.experimental import pallas as pl
from jax.experimental.pallas import tpu as pltpu
from jax.sharding import PartitionSpec as P

REACH = 2
MESH = pl.DeviceIdType.MESH
NCORE, NX, NY, NZH = 2, 4, 4, 2
GROUP = 4


def halos(block, axis, width):
    count = lax.axis_size(axis)
    forward = [(i, i + 1) for i in range(count - 1)]
    backward = [(target, source) for source, target in forward]
    low = lax.ppermute(block[-width:], axis, forward)
    high = lax.ppermute(block[:width], axis, backward)
    return low, high


def scatter_kernel(scale, p_ref, o_ref, pair_in, plane_out, plane_in, line_out, line_in, sems0, s1, r1, s2, r2):
    m = lax.axis_index("mesh")
    c = lax.axis_index("col")
    core = m % NCORE
    x = (m // NCORE) % NX
    y = (m // (NCORE * NX)) % NY
    zh = m // (NCORE * NX * NY)
    ncol = line_out.shape[0] // NZH
    nplane, nline = NX * NY, NZH * ncol
    rows = p_ref.shape[2] // NZH
    wide = p_ref.shape[3] // ncol
    z = zh * ncol + c

    def plane_peer(k):
        px = (x + k % NX) % NX
        py = (y + k // NX) % NY
        return py * NX + px, (((zh * NY + py) * NX + px) * NCORE + core, c)

    def line_peer(k):
        pz = (z + k) % nline
        return pz, ((pz // ncol) * (NCORE * NX * NY) + m % (NCORE * NX * NY), pz % ncol)

    pair = (m + 1 - 2 * core, c)

    barrier = pltpu.get_barrier_semaphore()
    pl.semaphore_signal(barrier, inc=1, device_id=pair, device_id_type=MESH)
    for k in range(1, nplane):
        pl.semaphore_signal(barrier, inc=1, device_id=plane_peer(k)[1], device_id_type=MESH)
    for k in range(1, nline):
        pl.semaphore_signal(barrier, inc=1, device_id=line_peer(k)[1], device_id_type=MESH)
    pl.semaphore_wait(barrier, 1 + (nplane - 1) + (nline - 1))

    copy0 = pltpu.make_async_remote_copy(
        src_ref=p_ref.at[1 - core], dst_ref=pair_in, send_sem=sems0.at[0], recv_sem=sems0.at[1],
        device_id=pair, device_id_type=MESH,
    )
    copy0.start()
    copy0.wait()

    copies1 = []
    for k in range(1, nplane):
        j, dev = plane_peer(k)
        plane_out[j] = (p_ref[core, j].astype(jnp.float32) + pair_in[j].astype(jnp.float32)).astype(plane_out.dtype)
        copy = pltpu.make_async_remote_copy(
            src_ref=plane_out.at[j], dst_ref=plane_in.at[k - 1], send_sem=s1.at[k - 1], recv_sem=r1.at[k - 1],
            device_id=dev, device_id_type=MESH,
        )
        copy.start()
        copies1.append(copy)
    own = y * NX + x
    acc = p_ref[core, own].astype(jnp.float32) + pair_in[own].astype(jnp.float32)
    for k in range(1, nplane):
        copies1[k - 1].wait_recv()
        acc += plane_in[k - 1].astype(jnp.float32)

    for h in range(NZH):
        for q in range(ncol):
            line_out[h * ncol + q] = acc[h * rows:(h + 1) * rows, q * wide:(q + 1) * wide]
    copies2 = []
    for k in range(1, nline):
        j, dev = line_peer(k)
        copy = pltpu.make_async_remote_copy(
            src_ref=line_out.at[j], dst_ref=line_in.at[k - 1], send_sem=s2.at[k - 1], recv_sem=r2.at[k - 1],
            device_id=dev, device_id_type=MESH,
        )
        copy.start()
        copies2.append(copy)
    total = line_out[z]
    for k in range(1, nline):
        copies2[k - 1].wait_recv()
        total += line_in[k - 1]
    o_ref[...] = total * scale
    for copy in copies1 + copies2:
        copy.wait_send()


def dense_kernel(low_ref, basis_ref, high_ref, jac_ref, cols_ref, live_ref, acc_ref, image_ref, part_ref, pad, top, rest, sem):
    nblk, slots, bs, _ = jac_ref.shape
    width = basis_ref.shape[1]
    reach = low_ref.shape[0]
    nrows = nblk * bs
    span = GROUP * bs + 2 * reach
    lanes = 2 * bs
    first = (lax.axis_index("mesh") * lax.axis_size("col") + lax.axis_index("col")) * nblk
    moves = [
        pltpu.make_async_copy(low_ref, pad.at[pl.ds(0, reach)], sem.at[0]),
        pltpu.make_async_copy(basis_ref, pad.at[pl.ds(reach, nrows)], sem.at[1]),
        pltpu.make_async_copy(high_ref, pad.at[pl.ds(reach + nrows, reach)], sem.at[2]),
    ]
    for move in moves:
        move.start()
    left = lax.broadcasted_iota(jnp.int32, (1, lanes), 1) < bs
    lane = lax.broadcasted_iota(jnp.int32, (bs, lanes), 1)
    row = lax.broadcasted_iota(jnp.int32, (bs, lanes), 0)

    def build(g, carry):
        for i in range(GROUP):
            r = g * GROUP + i
            own = first + r
            place = [jnp.where(s < live_ref[r], cols_ref[s, r] - own + REACH, -slots) for s in range(slots)]
            tiles = [jnp.zeros((bs, lanes), jnp.float32) for _ in range(3)]
            for p in range(0, slots, 2):
                a, b = jac_ref[r, p], jac_ref[r, p + 1]
                straight = jnp.concatenate([a, b], axis=1).astype(jnp.float32)
                crossed = jnp.concatenate([b, a], axis=1).astype(jnp.float32)
                where_s = jnp.where(left, place[p], place[p + 1])
                where_c = jnp.where(left, place[p + 1], place[p])
                for t in range(3):
                    w = 2 * (t + i // 2) - i
                    goal = jnp.where(left, w, w + 1)
                    tiles[t] += straight * (where_s == goal).astype(jnp.float32)
                    tiles[t] += crossed * (where_c == goal).astype(jnp.float32)
            t = (i + REACH) // 2 - i // 2
            gains = acc_ref[pl.ds(g * (GROUP // 2) + i // 2, 1), :]
            tiles[t] += jnp.where(lane == row + bs * (i % 2), gains, 0.0)
            for t in range(span // lanes):
                k = t - i // 2
                here = (g, pl.ds(i * bs, bs), pl.ds(t * lanes, lanes))
                if 0 <= k < 3:
                    big = tiles[k].astype(jnp.bfloat16)
                    top[here] = big
                    rest[here] = (tiles[k] - big.astype(jnp.float32)).astype(jnp.bfloat16)
                else:
                    top[here] = jnp.zeros((bs, lanes), jnp.bfloat16)
                    rest[here] = jnp.zeros((bs, lanes), jnp.bfloat16)
        return carry

    lax.fori_loop(0, nblk // GROUP, build, 0)
    for move in moves:
        move.wait()

    def apply(g, carry):
        rows = GROUP * bs
        window = pad[pl.ds(pl.multiple_of(g * rows, rows), span), :]
        out = jnp.dot(top[g], window, preferred_element_type=jnp.float32)
        out += jnp.dot(rest[g], window, preferred_element_type=jnp.float32)
        image_ref[pl.ds(pl.multiple_of(g * rows, rows), rows), :] = out.astype(image_ref.dtype)
        return carry

    lax.fori_loop(0, nblk // GROUP, apply, 0)

    part = lax.dot_general(
        pad[pl.ds(reach, nrows), :], image_ref[...], (((0,), (0,)), ((), ())), preferred_element_type=jnp.float32
    )
    ncore, nplane, both, _ = part_ref.shape
    rows = both // NZH
    for core in range(ncore):
        for j in range(nplane):
            for h in range(NZH):
                at = ((h * nplane + j) * ncore + core) * rows
                part_ref[core, j, h * rows:(h + 1) * rows] = part[at:at + rows].astype(part_ref.dtype)


def dense(basis, low, high, jac_blocks, block_cols, live_slots, accumulation):
    nrows, width = basis.shape
    nblk, slots, bs, _ = jac_blocks.shape
    nplane = NX * NY
    rows = width // lax.axis_size("mesh")
    span = (GROUP + 2 * REACH) * bs
    ngroup = nblk // GROUP
    any_spec = pl.BlockSpec(memory_space=pl.ANY)
    vmem = pl.BlockSpec(memory_space=pltpu.VMEM)
    smem = pl.BlockSpec(memory_space=pltpu.SMEM)
    return pl.pallas_call(
        dense_kernel,
        out_shape=(
            jax.ShapeDtypeStruct((nrows, width), jnp.bfloat16),
            jax.ShapeDtypeStruct((NCORE, nplane, NZH * rows, width), jnp.bfloat16),
        ),
        in_specs=[any_spec, any_spec, any_spec, vmem, smem, smem, vmem],
        out_specs=(vmem, vmem),
        scratch_shapes=[
            pltpu.VMEM((nrows + 2 * REACH * bs, width), jnp.bfloat16),
            pltpu.VMEM((ngroup, GROUP * bs, span), jnp.bfloat16),
            pltpu.VMEM((ngroup, GROUP * bs, span), jnp.bfloat16),
            pltpu.SemaphoreType.DMA((3,)),
        ],
        compiler_params=pltpu.CompilerParams(vmem_limit_bytes=40 << 20),
    )(low, basis, high, jac_blocks, block_cols.T, live_slots, accumulation.reshape(nrows // (2 * bs), 2 * bs))


def scatter_sum(p, scale, rows, wide):
    ncore, nplane, both, ncols = p.shape
    nline = NZH * (ncols // wide)
    return pl.pallas_call(
        functools.partial(scatter_kernel, scale),
        out_shape=jax.ShapeDtypeStruct((rows, wide), jnp.float32),
        in_specs=[pl.BlockSpec(memory_space=pltpu.VMEM)],
        out_specs=pl.BlockSpec(memory_space=pltpu.VMEM),
        scratch_shapes=[
            pltpu.VMEM((nplane, both, ncols), jnp.bfloat16),
            pltpu.VMEM((nplane, both, ncols), jnp.bfloat16),
            pltpu.VMEM((nplane - 1, both, ncols), jnp.bfloat16),
            pltpu.VMEM((nline, rows, wide), jnp.float32),
            pltpu.VMEM((nline - 1, rows, wide), jnp.float32),
            pltpu.SemaphoreType.DMA((2,)),
            pltpu.SemaphoreType.DMA((nplane - 1,)),
            pltpu.SemaphoreType.DMA((nplane - 1,)),
            pltpu.SemaphoreType.DMA((nline - 1,)),
            pltpu.SemaphoreType.DMA((nline - 1,)),
        ],
        compiler_params=pltpu.CompilerParams(collective_id=0, has_side_effects=True),
    )(p)


def local(basis, jac_blocks, block_cols, live_slots, accumulation):
    nrows, width = basis.shape
    bs = jac_blocks.shape[2]
    mesh_count, col_count = lax.axis_size("mesh"), lax.axis_size("col")
    low, high = halos(basis, ("mesh", "col"), REACH * bs)
    image, part = dense(basis, low, high, jac_blocks, block_cols, live_slots, accumulation)
    scale = 1.0 / (nrows * mesh_count * col_count)
    projected = scatter_sum(part, scale, width // mesh_count, width // col_count)
    return (image, projected)


def solution(mesh):
    return jax.shard_map(
        local,
        mesh=mesh,
        in_specs=(
            P(("mesh", "col"), None),
            P(("mesh", "col"), None, None, None),
            P(("mesh", "col"), None),
            P(("mesh", "col")),
            P(("mesh", "col")),
        ),
        out_specs=(P(("mesh", "col"), None), P("mesh", "col")),
        check_vma=False,
    )
```

```python
import functools

import jax
import jax.numpy as jnp
from jax import lax
from jax.experimental import pallas as pl
from jax.experimental.pallas import tpu as pltpu
from jax.sharding import PartitionSpec as P

REACH = 2
GROUP = 4
MESH = pl.DeviceIdType.MESH
NCORE, NX, NY, NZH = 2, 4, 4, 2
PIECES = 4


def hops(step, size):
    return min(step, size - step)


PLANE = sorted(
    ((dx, dy) for dx in range(NX) for dy in range(NY)), key=lambda d: -hops(d[0], NX) - hops(d[1], NY)
)


def kernel(
    basis_ref, jac_ref, cols_ref, live_ref, acc_ref, image_ref, total_ref,
    pad, jac, cols, live, gain, top, rest, part, pair_out, pair_in, plane_out, plane_in, line_out, line_in,
    local_sem, halo_send, halo_recv, s0, r0, s1, r1, s2, r2,
):
    m, c = lax.axis_index("mesh"), lax.axis_index("col")
    nm, nc = lax.axis_size("mesh"), lax.axis_size("col")
    core = m % NCORE
    x = (m // NCORE) % NX
    y = (m // (NCORE * NX)) % NY
    zh = m // (NCORE * NX * NY)
    z = zh * nc + c
    nplane, nline = NX * NY, NZH * nc
    line_steps = sorted(range(1, nline), key=lambda k: -hops(k, nline))

    nblk, slots, bs, _ = jac.shape
    nrows, width = basis_ref.shape
    reach = REACH * bs
    span = GROUP * bs + 2 * reach
    lanes = 2 * bs
    rows = total_ref.shape[0]
    wide = total_ref.shape[1]

    def plane_peer(step):
        px, py = (x + step[0]) % NX, (y + step[1]) % NY
        return py * NX + px, (((zh * NY + py) * NX + px) * NCORE + core, c)

    def line_peer(k):
        pz = (z + k) % nline
        return pz, ((pz // nc) * (NCORE * NX * NY) + m % (NCORE * NX * NY), pz % nc)

    index = m * nc + c
    before, after = (index + nm * nc - 1) % (nm * nc), (index + 1) % (nm * nc)
    low_peer, high_peer = (before // nc, before % nc), (after // nc, after % nc)
    pair = (m + 1 - 2 * core, c)

    moves = [
        pltpu.make_async_copy(cols_ref, cols, local_sem.at[0]),
        pltpu.make_async_copy(live_ref, live, local_sem.at[1]),
        pltpu.make_async_copy(acc_ref, gain, local_sem.at[2]),
        pltpu.make_async_copy(jac_ref, jac, local_sem.at[3]),
        pltpu.make_async_copy(basis_ref, pad.at[pl.ds(reach, nrows)], local_sem.at[4]),
    ]
    for move in moves:
        move.start()

    barrier = pltpu.get_barrier_semaphore()
    peers = [low_peer, high_peer] + [line_peer(k)[1] for k in line_steps]
    peers += [plane_peer(step)[1] for step in PLANE[:-1]] + [pair]
    for peer in peers:
        pl.semaphore_signal(barrier, inc=1, device_id=peer, device_id_type=MESH)

    for move in moves[:4]:
        move.wait()

    first = index * nblk
    left = lax.broadcasted_iota(jnp.int32, (1, lanes), 1) < bs
    lane = lax.broadcasted_iota(jnp.int32, (bs, lanes), 1)
    row = lax.broadcasted_iota(jnp.int32, (bs, lanes), 0)

    def build(g, carry):
        for i in range(GROUP):
            r = g * GROUP + i
            own = first + r
            place = [jnp.where(s < live[r], cols[s, r] - own + REACH, -slots) for s in range(slots)]
            tiles = [jnp.zeros((bs, lanes), jnp.float32) for _ in range(3)]
            for p in range(0, slots, 2):
                a, b = jac[r, p], jac[r, p + 1]
                straight = jnp.concatenate([a, b], axis=1).astype(jnp.float32)
                crossed = jnp.concatenate([b, a], axis=1).astype(jnp.float32)
                where_s = jnp.where(left, place[p], place[p + 1])
                where_c = jnp.where(left, place[p + 1], place[p])
                for t in range(3):
                    w = 2 * (t + i // 2) - i
                    goal = jnp.where(left, w, w + 1)
                    tiles[t] += straight * (where_s == goal).astype(jnp.float32)
                    tiles[t] += crossed * (where_c == goal).astype(jnp.float32)
            t = (i + REACH) // 2 - i // 2
            gains = gain[pl.ds(g * (GROUP // 2) + i // 2, 1), :]
            tiles[t] += jnp.where(lane == row + bs * (i % 2), gains, 0.0)
            for t in range(span // lanes):
                k = t - i // 2
                here = (g, pl.ds(i * bs, bs), pl.ds(t * lanes, lanes))
                if 0 <= k < 3:
                    big = tiles[k].astype(jnp.bfloat16)
                    top[here] = big
                    rest[here] = (tiles[k] - big.astype(jnp.float32)).astype(jnp.bfloat16)
                else:
                    top[here] = jnp.zeros((bs, lanes), jnp.bfloat16)
                    rest[here] = jnp.zeros((bs, lanes), jnp.bfloat16)
        return carry

    ngroup = nblk // GROUP
    lax.fori_loop(0, ngroup, build, 0)
    moves[4].wait()

    pl.semaphore_wait(barrier, len(peers))
    up = pltpu.make_async_remote_copy(
        src_ref=pad.at[pl.ds(nrows, reach)], dst_ref=pad.at[pl.ds(0, reach)],
        send_sem=halo_send.at[0], recv_sem=halo_recv.at[0], device_id=high_peer, device_id_type=MESH,
    )
    down = pltpu.make_async_remote_copy(
        src_ref=pad.at[pl.ds(reach, reach)], dst_ref=pad.at[pl.ds(reach + nrows, reach)],
        send_sem=halo_send.at[1], recv_sem=halo_recv.at[1], device_id=low_peer, device_id_type=MESH,
    )
    up.start()
    down.start()

    step = GROUP * bs

    def apply(g, carry):
        at = pl.multiple_of(g * step, step)
        window = pad[pl.ds(at, span), :]
        out = jnp.dot(top[g], window, preferred_element_type=jnp.float32)
        out += jnp.dot(rest[g], window, preferred_element_type=jnp.float32)
        image_ref[pl.ds(at, step), :] = out.astype(image_ref.dtype)
        return carry

    def project(start, size):
        return lax.dot_general(
            pad[pl.ds(reach + start, size), :], image_ref[pl.ds(start, size), :],
            (((0,), (0,)), ((), ())), preferred_element_type=jnp.float32,
        )

    lax.fori_loop(1, ngroup - 1, apply, 0)
    part[...] = project(step, nrows - 2 * step)
    up.wait()
    down.wait()
    apply(0, 0)
    apply(ngroup - 1, 0)
    part[...] += project(0, step) + project(nrows - step, step)

    def share(j, which):
        at = [pl.multiple_of(((h * nplane + j) * NCORE + which) * rows, rows) for h in range(NZH)]
        return jnp.concatenate([part[pl.ds(a, rows), :] for a in at], axis=0)

    each = nplane // PIECES
    swaps = []
    for q in range(PIECES):
        for n in range(q * each, (q + 1) * each):
            pair_out[n] = share(plane_peer(PLANE[n])[0], 1 - core).astype(pair_out.dtype)
        swap = pltpu.make_async_remote_copy(
            src_ref=pair_out.at[pl.ds(q * each, each)], dst_ref=pair_in.at[pl.ds(q * each, each)],
            send_sem=s0.at[q], recv_sem=r0.at[q], device_id=pair, device_id_type=MESH,
        )
        swap.start()
        swaps.append(swap)

    sent = []
    acc = None
    for q in range(PIECES):
        swaps[q].wait_recv()
        for n in range(q * each, (q + 1) * each):
            j, peer = plane_peer(PLANE[n])
            both = share(j, core) + pair_in[n].astype(jnp.float32)
            if n == nplane - 1:
                acc = both
                continue
            plane_out[n] = both.astype(plane_out.dtype)
            copy = pltpu.make_async_remote_copy(
                src_ref=plane_out.at[n], dst_ref=plane_in.at[n], send_sem=s1.at[n], recv_sem=r1.at[n],
                device_id=peer, device_id_type=MESH,
            )
            copy.start()
            sent.append(copy)
    for n in reversed(range(nplane - 1)):
        sent[n].wait_recv()
        acc += plane_in[n].astype(jnp.float32)

    for h in range(NZH):
        for q in range(nc):
            line_out[h * nc + q] = acc[h * rows:(h + 1) * rows, q * wide:(q + 1) * wide]
    last = []
    for n, k in enumerate(line_steps):
        j, peer = line_peer(k)
        copy = pltpu.make_async_remote_copy(
            src_ref=line_out.at[j], dst_ref=line_in.at[n], send_sem=s2.at[n], recv_sem=r2.at[n],
            device_id=peer, device_id_type=MESH,
        )
        copy.start()
        last.append(copy)
    total = line_out[z]
    for n in reversed(range(nline - 1)):
        last[n].wait_recv()
        total += line_in[n]
    total_ref[...] = total
    for copy in swaps + sent + last:
        copy.wait_send()


def local(basis, jac_blocks, block_cols, live_slots, accumulation):
    nrows, width = basis.shape
    nblk, slots, bs, _ = jac_blocks.shape
    mesh_count, col_count = lax.axis_size("mesh"), lax.axis_size("col")
    rows, wide = width // mesh_count, width // col_count
    nplane, nline = NX * NY, NZH * col_count
    span = (GROUP + 2 * REACH) * bs
    ngroup = nblk // GROUP
    lanes = 2 * bs
    image, total = pl.pallas_call(
        kernel,
        out_shape=(
            jax.ShapeDtypeStruct((nrows, width), jnp.bfloat16),
            jax.ShapeDtypeStruct((rows, wide), jnp.float32),
        ),
        in_specs=[pl.BlockSpec(memory_space=pl.ANY)] * 5,
        out_specs=(pl.BlockSpec(memory_space=pltpu.VMEM), pl.BlockSpec(memory_space=pltpu.VMEM)),
        scratch_shapes=[
            pltpu.VMEM((nrows + 2 * REACH * bs, width), jnp.bfloat16),
            pltpu.VMEM((nblk, slots, bs, bs), jnp.bfloat16),
            pltpu.SMEM((slots, nblk), jnp.int32),
            pltpu.SMEM((nblk,), jnp.int32),
            pltpu.VMEM((nrows // lanes, lanes), jnp.float32),
            pltpu.VMEM((ngroup, GROUP * bs, span), jnp.bfloat16),
            pltpu.VMEM((ngroup, GROUP * bs, span), jnp.bfloat16),
            pltpu.VMEM((width, width), jnp.float32),
            pltpu.VMEM((nplane, NZH * rows, width), jnp.bfloat16),
            pltpu.VMEM((nplane, NZH * rows, width), jnp.bfloat16),
            pltpu.VMEM((nplane - 1, NZH * rows, width), jnp.bfloat16),
            pltpu.VMEM((nplane - 1, NZH * rows, width), jnp.bfloat16),
            pltpu.VMEM((nline, rows, wide), jnp.float32),
            pltpu.VMEM((nline - 1, rows, wide), jnp.float32),
            pltpu.SemaphoreType.DMA((5,)),
            pltpu.SemaphoreType.DMA((2,)),
            pltpu.SemaphoreType.DMA((2,)),
            pltpu.SemaphoreType.DMA((PIECES,)),
            pltpu.SemaphoreType.DMA((PIECES,)),
            pltpu.SemaphoreType.DMA((nplane - 1,)),
            pltpu.SemaphoreType.DMA((nplane - 1,)),
            pltpu.SemaphoreType.DMA((nline - 1,)),
            pltpu.SemaphoreType.DMA((nline - 1,)),
        ],
        compiler_params=pltpu.CompilerParams(
            collective_id=0, has_side_effects=True, vmem_limit_bytes=56 << 20
        ),
    )(basis, jac_blocks, block_cols.T, live_slots, accumulation.reshape(nrows // lanes, lanes))
    projected = total * (1.0 / (nrows * mesh_count * col_count))
    return (image, projected)


def solution(mesh):
    return jax.shard_map(
        local,
        mesh=mesh,
        in_specs=(
            P(("mesh", "col"), None),
            P(("mesh", "col"), None, None, None),
            P(("mesh", "col"), None),
            P(("mesh", "col")),
            P(("mesh", "col")),
        ),
        out_specs=(P(("mesh", "col"), None), P("mesh", "col")),
        check_vma=False,
    )
```

```python
import functools

import jax
import jax.numpy as jnp
from jax import lax
from jax.experimental import pallas as pl
from jax.experimental.pallas import tpu as pltpu
from jax.sharding import PartitionSpec as P

REACH = 2
GROUP = 4
MESH = pl.DeviceIdType.MESH
NCORE, NX, NY, NZH = 2, 4, 4, 2
PIECES = 4
WRITES = 6


def hops(step, size):
    return min(step, size - step)


PLANE = sorted(
    ((dx, dy) for dx in range(NX) for dy in range(NY)), key=lambda d: -hops(d[0], NX) - hops(d[1], NY)
)


def kernel(
    basis_ref, jac_ref, cols_ref, live_ref, acc_ref, image_ref, total_ref,
    pad, jac, cols, live, gain, top, rest, part, pair_out, pair_in, plane_out, plane_in, line_out, line_in,
    local_sem, jac_sem, basis_sem, halo_send, halo_recv, s0, r0, s1, r1, s2, r2,
):
    m, c = lax.axis_index("mesh"), lax.axis_index("col")
    nm, nc = lax.axis_size("mesh"), lax.axis_size("col")
    core = m % NCORE
    x = (m // NCORE) % NX
    y = (m // (NCORE * NX)) % NY
    zh = m // (NCORE * NX * NY)
    z = zh * nc + c
    nplane, nline = NX * NY, NZH * nc
    line_steps = sorted(range(1, nline), key=lambda k: -hops(k, nline))

    nblk, slots, bs, _ = jac.shape
    nrows, width = basis_ref.shape
    reach = REACH * bs
    span = GROUP * bs + 2 * reach
    lanes = 2 * bs
    step = GROUP * bs
    ngroup = nblk // GROUP
    rows = total_ref.shape[0]
    wide = total_ref.shape[1]

    def plane_peer(step):
        px, py = (x + step[0]) % NX, (y + step[1]) % NY
        return py * NX + px, (((zh * NY + py) * NX + px) * NCORE + core, c)

    def line_peer(k):
        pz = (z + k) % nline
        return pz, ((pz // nc) * (NCORE * NX * NY) + m % (NCORE * NX * NY), pz % nc)

    index = m * nc + c
    before, after = (index + nm * nc - 1) % (nm * nc), (index + 1) % (nm * nc)
    low_peer, high_peer = (before // nc, before % nc), (after // nc, after % nc)
    pair = (m + 1 - 2 * core, c)

    moves = [
        pltpu.make_async_copy(cols_ref, cols, local_sem.at[0]),
        pltpu.make_async_copy(live_ref, live, local_sem.at[1]),
        pltpu.make_async_copy(acc_ref, gain, local_sem.at[2]),
    ]

    def jac_move(g):
        part_of = pl.ds(g * GROUP, GROUP)
        return pltpu.make_async_copy(jac_ref.at[part_of], jac.at[part_of], jac_sem.at[g])

    def basis_move(g):
        return pltpu.make_async_copy(
            basis_ref.at[pl.ds(g * step, step)], pad.at[pl.ds(reach + g * step, step)], basis_sem.at[g]
        )

    for move in moves:
        move.start()
    for g in range(ngroup):
        jac_move(g).start()
    for g in range(ngroup):
        basis_move(g).start()

    barrier = pltpu.get_barrier_semaphore()
    peers = [low_peer, high_peer] + [line_peer(k)[1] for k in line_steps]
    peers += [plane_peer(step)[1] for step in PLANE[:-1]] + [pair]
    for peer in peers:
        pl.semaphore_signal(barrier, inc=1, device_id=peer, device_id_type=MESH)

    for move in moves:
        move.wait()

    first = index * nblk
    left = lax.broadcasted_iota(jnp.int32, (1, lanes), 1) < bs
    lane = lax.broadcasted_iota(jnp.int32, (bs, lanes), 1)
    row = lax.broadcasted_iota(jnp.int32, (bs, lanes), 0)

    def build(g, carry):
        jac_move(g).wait()
        for i in range(GROUP):
            r = g * GROUP + i
            own = first + r
            place = [jnp.where(s < live[r], cols[s, r] - own + REACH, -slots) for s in range(slots)]
            tiles = [jnp.zeros((bs, lanes), jnp.float32) for _ in range(3)]
            for p in range(0, slots, 2):
                a, b = jac[r, p], jac[r, p + 1]
                straight = jnp.concatenate([a, b], axis=1).astype(jnp.float32)
                crossed = jnp.concatenate([b, a], axis=1).astype(jnp.float32)
                where_s = jnp.where(left, place[p], place[p + 1])
                where_c = jnp.where(left, place[p + 1], place[p])
                for t in range(3):
                    w = 2 * (t + i // 2) - i
                    goal = jnp.where(left, w, w + 1)
                    tiles[t] += straight * (where_s == goal).astype(jnp.float32)
                    tiles[t] += crossed * (where_c == goal).astype(jnp.float32)
            t = (i + REACH) // 2 - i // 2
            gains = gain[pl.ds(g * (GROUP // 2) + i // 2, 1), :]
            tiles[t] += jnp.where(lane == row + bs * (i % 2), gains, 0.0)
            for t in range(span // lanes):
                k = t - i // 2
                here = (g, pl.ds(i * bs, bs), pl.ds(t * lanes, lanes))
                if 0 <= k < 3:
                    big = tiles[k].astype(jnp.bfloat16)
                    top[here] = big
                    rest[here] = (tiles[k] - big.astype(jnp.float32)).astype(jnp.bfloat16)
                else:
                    top[here] = jnp.zeros((bs, lanes), jnp.bfloat16)
                    rest[here] = jnp.zeros((bs, lanes), jnp.bfloat16)
        return carry

    lax.fori_loop(0, ngroup, build, 0)
    for g in range(ngroup):
        basis_move(g).wait()

    pl.semaphore_wait(barrier, len(peers))
    up = pltpu.make_async_remote_copy(
        src_ref=pad.at[pl.ds(nrows, reach)], dst_ref=pad.at[pl.ds(0, reach)],
        send_sem=halo_send.at[0], recv_sem=halo_recv.at[0], device_id=high_peer, device_id_type=MESH,
    )
    down = pltpu.make_async_remote_copy(
        src_ref=pad.at[pl.ds(reach, reach)], dst_ref=pad.at[pl.ds(reach + nrows, reach)],
        send_sem=halo_send.at[1], recv_sem=halo_recv.at[1], device_id=low_peer, device_id_type=MESH,
    )
    up.start()
    down.start()

    def apply(g, carry):
        at = pl.multiple_of(g * step, step)
        window = pad[pl.ds(at, span), :]
        out = jnp.dot(top[g], window, preferred_element_type=jnp.float32)
        out += jnp.dot(rest[g], window, preferred_element_type=jnp.float32)
        image_ref[pl.ds(at, step), :] = out.astype(image_ref.dtype)
        return carry

    def project(start, size):
        return lax.dot_general(
            pad[pl.ds(reach + start, size), :], image_ref[pl.ds(start, size), :],
            (((0,), (0,)), ((), ())), preferred_element_type=jnp.float32,
        )

    lax.fori_loop(1, ngroup - 1, apply, 0)
    part[...] = project(step, nrows - 2 * step)
    up.wait()
    down.wait()
    apply(0, 0)
    apply(ngroup - 1, 0)
    part[...] += project(0, step) + project(nrows - step, step)

    def share(j, which):
        at = [pl.multiple_of(((h * nplane + j) * NCORE + which) * rows, rows) for h in range(NZH)]
        return jnp.concatenate([part[pl.ds(a, rows), :] for a in at], axis=0)

    each = nplane // PIECES
    swaps = []
    for q in range(PIECES):
        for n in range(q * each, (q + 1) * each):
            pair_out[n] = share(plane_peer(PLANE[n])[0], 1 - core).astype(pair_out.dtype)
        swap = pltpu.make_async_remote_copy(
            src_ref=pair_out.at[pl.ds(q * each, each)], dst_ref=pair_in.at[pl.ds(q * each, each)],
            send_sem=s0.at[q], recv_sem=r0.at[q], device_id=pair, device_id_type=MESH,
        )
        swap.start()
        swaps.append(swap)

    sent = []
    acc = None
    for q in range(PIECES):
        swaps[q].wait_recv()
        for n in range(q * each, (q + 1) * each):
            j, peer = plane_peer(PLANE[n])
            both = share(j, core) + pair_in[n].astype(jnp.float32)
            if n == nplane - 1:
                acc = both
                continue
            plane_out[n] = both.astype(plane_out.dtype)
            copy = pltpu.make_async_remote_copy(
                src_ref=plane_out.at[n], dst_ref=plane_in.at[n], send_sem=s1.at[n], recv_sem=r1.at[n],
                device_id=peer, device_id_type=MESH,
            )
            copy.start()
            sent.append(copy)
    for n in reversed(range(nplane - 1)):
        sent[n].wait_recv()
        acc += plane_in[n].astype(jnp.float32)

    for h in range(NZH):
        for q in range(nc):
            line_out[h * nc + q] = acc[h * rows:(h + 1) * rows, q * wide:(q + 1) * wide]
    last = []
    for n, k in enumerate(line_steps):
        j, peer = line_peer(k)
        copy = pltpu.make_async_remote_copy(
            src_ref=line_out.at[j], dst_ref=line_in.at[n], send_sem=s2.at[n], recv_sem=r2.at[n],
            device_id=peer, device_id_type=MESH,
        )
        copy.start()
        last.append(copy)
    total = line_out[z]
    for n in reversed(range(nline - 1)):
        last[n].wait_recv()
        total += line_in[n]
    total_ref[...] = total
    for copy in swaps + sent + last:
        copy.wait_send()


def finish(scale, image_ref, total_ref, image_out, projected_out, scaled, sem):
    size = image_ref.shape[0] // WRITES
    writes = [
        pltpu.make_async_copy(
            image_ref.at[pl.ds(q * size, size)], image_out.at[pl.ds(q * size, size)], sem.at[q]
        )
        for q in range(WRITES)
    ]
    for write in writes:
        write.start()
    scaled[...] = total_ref[...] * scale
    small = pltpu.make_async_copy(scaled, projected_out, sem.at[WRITES])
    small.start()
    for write in writes + [small]:
        write.wait()


def local(basis, jac_blocks, block_cols, live_slots, accumulation):
    nrows, width = basis.shape
    nblk, slots, bs, _ = jac_blocks.shape
    mesh_count, col_count = lax.axis_size("mesh"), lax.axis_size("col")
    rows, wide = width // mesh_count, width // col_count
    nplane, nline = NX * NY, NZH * col_count
    span = (GROUP + 2 * REACH) * bs
    ngroup = nblk // GROUP
    lanes = 2 * bs
    image, total = pl.pallas_call(
        kernel,
        out_shape=(
            pltpu.VMEM((nrows, width), jnp.bfloat16),
            pltpu.VMEM((rows, wide), jnp.float32),
        ),
        in_specs=[pl.BlockSpec(memory_space=pl.ANY)] * 5,
        out_specs=(pl.BlockSpec(memory_space=pltpu.VMEM), pl.BlockSpec(memory_space=pltpu.VMEM)),
        scratch_shapes=[
            pltpu.VMEM((nrows + 2 * REACH * bs, width), jnp.bfloat16),
            pltpu.VMEM((nblk, slots, bs, bs), jnp.bfloat16),
            pltpu.SMEM((slots, nblk), jnp.int32),
            pltpu.SMEM((nblk,), jnp.int32),
            pltpu.VMEM((nrows // lanes, lanes), jnp.float32),
            pltpu.VMEM((ngroup, GROUP * bs, span), jnp.bfloat16),
            pltpu.VMEM((ngroup, GROUP * bs, span), jnp.bfloat16),
            pltpu.VMEM((width, width), jnp.float32),
            pltpu.VMEM((nplane, NZH * rows, width), jnp.bfloat16),
            pltpu.VMEM((nplane, NZH * rows, width), jnp.bfloat16),
            pltpu.VMEM((nplane - 1, NZH * rows, width), jnp.bfloat16),
            pltpu.VMEM((nplane - 1, NZH * rows, width), jnp.bfloat16),
            pltpu.VMEM((nline, rows, wide), jnp.float32),
            pltpu.VMEM((nline - 1, rows, wide), jnp.float32),
            pltpu.SemaphoreType.DMA((3,)),
            pltpu.SemaphoreType.DMA((ngroup,)),
            pltpu.SemaphoreType.DMA((ngroup,)),
            pltpu.SemaphoreType.DMA((2,)),
            pltpu.SemaphoreType.DMA((2,)),
            pltpu.SemaphoreType.DMA((PIECES,)),
            pltpu.SemaphoreType.DMA((PIECES,)),
            pltpu.SemaphoreType.DMA((nplane - 1,)),
            pltpu.SemaphoreType.DMA((nplane - 1,)),
            pltpu.SemaphoreType.DMA((nline - 1,)),
            pltpu.SemaphoreType.DMA((nline - 1,)),
        ],
        compiler_params=pltpu.CompilerParams(
            collective_id=0, has_side_effects=True, vmem_limit_bytes=56 << 20
        ),
    )(basis, jac_blocks, block_cols.T, live_slots, accumulation.reshape(nrows // lanes, lanes))
    image = pltpu.with_memory_space_constraint(image, pltpu.VMEM)
    total = pltpu.with_memory_space_constraint(total, pltpu.VMEM)
    return pl.pallas_call(
        functools.partial(finish, 1.0 / (nrows * mesh_count * col_count)),
        out_shape=(
            jax.ShapeDtypeStruct((nrows, width), jnp.bfloat16),
            jax.ShapeDtypeStruct((rows, wide), jnp.float32),
        ),
        in_specs=[pl.BlockSpec(memory_space=pltpu.VMEM)] * 2,
        out_specs=(pl.BlockSpec(memory_space=pl.ANY), pl.BlockSpec(memory_space=pl.ANY)),
        scratch_shapes=[pltpu.VMEM((rows, wide), jnp.float32), pltpu.SemaphoreType.DMA((WRITES + 1,))],
    )(image, total)


def solution(mesh):
    return jax.shard_map(
        local,
        mesh=mesh,
        in_specs=(
            P(("mesh", "col"), None),
            P(("mesh", "col"), None, None, None),
            P(("mesh", "col"), None),
            P(("mesh", "col")),
            P(("mesh", "col")),
        ),
        out_specs=(P(("mesh", "col"), None), P("mesh", "col")),
        check_vma=False,
    )
```

```python
import functools

import jax
import jax.numpy as jnp
from jax import lax
from jax.experimental import pallas as pl
from jax.experimental.pallas import tpu as pltpu
from jax.sharding import PartitionSpec as P

REACH = 2
GROUP = 4
MESH = pl.DeviceIdType.MESH
NCORE, NX, NY, NZH = 2, 4, 4, 2
PIECES = 4
WRITES = 6
FAR = (1, 2, 4)


def hops(step, size):
    return min(step, size - step)


PLANE = sorted(
    ((dx, dy) for dx in range(NX) for dy in range(NY)), key=lambda d: -hops(d[0], NX) - hops(d[1], NY)
)


def kernel(
    basis_ref, jac_ref, cols_ref, live_ref, acc_ref, image_ref, total_ref,
    pad, jac, cols, live, gain, top, rest, part, pair_out, pair_in, plane_out, plane_in, line_out, line_in,
    local_sem, jac_sem, basis_sem, halo_send, halo_recv, known, s0, r0, s1, r1, s2, r2,
):
    m, c = lax.axis_index("mesh"), lax.axis_index("col")
    nm, nc = lax.axis_size("mesh"), lax.axis_size("col")
    core = m % NCORE
    x = (m // NCORE) % NX
    y = (m // (NCORE * NX)) % NY
    zh = m // (NCORE * NX * NY)
    z = zh * nc + c
    nplane, nline = NX * NY, NZH * nc
    line_steps = sorted(range(1, nline), key=lambda k: -hops(k, nline))

    nblk, slots, bs, _ = jac.shape
    nrows, width = basis_ref.shape
    reach = REACH * bs
    span = GROUP * bs + 2 * reach
    lanes = 2 * bs
    step = GROUP * bs
    ngroup = nblk // GROUP
    rows = total_ref.shape[0]
    wide = total_ref.shape[1]

    def plane_peer(step):
        px, py = (x + step[0]) % NX, (y + step[1]) % NY
        return py * NX + px, (((zh * NY + py) * NX + px) * NCORE + core, c)

    def line_peer(k):
        pz = (z + k) % nline
        return pz, ((pz // nc) * (NCORE * NX * NY) + m % (NCORE * NX * NY), pz % nc)

    index = m * nc + c
    before, after = (index + nm * nc - 1) % (nm * nc), (index + 1) % (nm * nc)
    low_peer, high_peer = (before // nc, before % nc), (after // nc, after % nc)
    pair = (m + 1 - 2 * core, c)

    moves = [
        pltpu.make_async_copy(cols_ref, cols, local_sem.at[0]),
        pltpu.make_async_copy(live_ref, live, local_sem.at[1]),
        pltpu.make_async_copy(acc_ref, gain, local_sem.at[2]),
    ]

    def jac_move(g):
        part_of = pl.ds(g * GROUP, GROUP)
        return pltpu.make_async_copy(jac_ref.at[part_of], jac.at[part_of], jac_sem.at[g])

    def basis_move(g):
        return pltpu.make_async_copy(
            basis_ref.at[pl.ds(g * step, step)], pad.at[pl.ds(reach + g * step, step)], basis_sem.at[g]
        )

    for move in moves:
        move.start()
    inner = ngroup - 2
    jac_move(1).start()
    for g in range(ngroup):
        basis_move(g).start()
    for g in [*range(2, ngroup - 1), 0, ngroup - 1]:
        jac_move(g).start()

    barrier = pltpu.get_barrier_semaphore()
    beside = [line_peer(1)[1], line_peer(nline - 1)[1]]
    peers = [low_peer, high_peer] + beside + [plane_peer(step)[1] for step in PLANE[:-1]] + [pair]
    for peer in peers:
        pl.semaphore_signal(barrier, inc=1, device_id=peer, device_id_type=MESH)

    for move in moves:
        move.wait()

    first = index * nblk
    left = lax.broadcasted_iota(jnp.int32, (1, lanes), 1) < bs
    lane = lax.broadcasted_iota(jnp.int32, (bs, lanes), 1)
    row = lax.broadcasted_iota(jnp.int32, (bs, lanes), 0)

    def build(g):
        for i in range(GROUP):
            r = g * GROUP + i
            own = first + r
            place = [jnp.where(s < live[r], cols[s, r] - own + REACH, -slots) for s in range(slots)]
            tiles = [jnp.zeros((bs, lanes), jnp.float32) for _ in range(3)]
            for p in range(0, slots, 2):
                a, b = jac[r, p], jac[r, p + 1]
                straight = jnp.concatenate([a, b], axis=1).astype(jnp.float32)
                crossed = jnp.concatenate([b, a], axis=1).astype(jnp.float32)
                where_s = jnp.where(left, place[p], place[p + 1])
                where_c = jnp.where(left, place[p + 1], place[p])
                for t in range(3):
                    w = 2 * (t + i // 2) - i
                    goal = jnp.where(left, w, w + 1)
                    tiles[t] += straight * (where_s == goal).astype(jnp.float32)
                    tiles[t] += crossed * (where_c == goal).astype(jnp.float32)
            t = (i + REACH) // 2 - i // 2
            gains = gain[pl.ds(g * (GROUP // 2) + i // 2, 1), :]
            tiles[t] += jnp.where(lane == row + bs * (i % 2), gains, 0.0)
            for t in range(span // lanes):
                k = t - i // 2
                here = (g, pl.ds(i * bs, bs), pl.ds(t * lanes, lanes))
                if 0 <= k < 3:
                    big = tiles[k].astype(jnp.bfloat16)
                    top[here] = big
                    rest[here] = (tiles[k] - big.astype(jnp.float32)).astype(jnp.bfloat16)
                else:
                    top[here] = jnp.zeros((bs, lanes), jnp.bfloat16)
                    rest[here] = jnp.zeros((bs, lanes), jnp.bfloat16)

    jac_move(1).wait()
    build(1)
    for g in range(ngroup):
        basis_move(g).wait()
    part[...] = jnp.zeros_like(part)

    up = pltpu.make_async_remote_copy(
        src_ref=pad.at[pl.ds(nrows, reach)], dst_ref=pad.at[pl.ds(0, reach)],
        send_sem=halo_send.at[0], recv_sem=halo_recv.at[0], device_id=high_peer, device_id_type=MESH,
    )
    down = pltpu.make_async_remote_copy(
        src_ref=pad.at[pl.ds(reach, reach)], dst_ref=pad.at[pl.ds(reach + nrows, reach)],
        send_sem=halo_send.at[1], recv_sem=halo_recv.at[1], device_id=low_peer, device_id_type=MESH,
    )
    meet_at = inner * jnp.where((z == 0) | (z == nline - 1), 1, 0)

    def tell(k):
        for peer in (line_peer(FAR[k])[1], line_peer(nline - FAR[k])[1]):
            pl.semaphore_signal(known.at[k], inc=1, device_id=peer, device_id_type=MESH)

    def hear(k):
        pl.semaphore_wait(known.at[k], 2)

    far_low = jnp.where(c == 0, 1, 0)

    def ends(k):
        return jnp.where(k == inner + far_low, 1, 0), jnp.where(k == inner + 1 - far_low, 1, 0)

    def order(k):
        low_now, high_now = ends(k)
        return (1 - low_now - high_now) * (k + 1) + high_now * (ngroup - 1)

    def ready(k):
        low_now, high_now = ends(k)

        @pl.when(k == meet_at)
        def _():
            pl.semaphore_wait(barrier, len(peers))
            up.start()
            down.start()
            tell(0)

        @pl.when(low_now == 1)
        def _():
            up.wait_recv()

        @pl.when(high_now == 1)
        def _():
            down.wait_recv()

    def multiply(g):
        at = pl.multiple_of(g * step, step)
        window = pad[pl.ds(at, span), :]
        out = jnp.dot(top[g], window, preferred_element_type=jnp.float32)
        out += jnp.dot(rest[g], window, preferred_element_type=jnp.float32)
        out = out.astype(image_ref.dtype)
        image_ref[pl.ds(at, step), :] = out
        part[...] += lax.dot_general(
            pad[pl.ds(reach + at, step), :], out, (((0,), (0,)), ((), ())), preferred_element_type=jnp.float32
        )

    def both(k, carry):
        ready(k)
        later = order(k + 1)
        jac_move(later).wait()
        multiply(order(k))
        build(later)
        return carry

    lax.fori_loop(0, ngroup - 1, both, 0)
    hear(0)
    tell(1)
    ready(ngroup - 1)
    multiply(order(ngroup - 1))

    def share(j, which):
        at = [pl.multiple_of(((h * nplane + j) * NCORE + which) * rows, rows) for h in range(NZH)]
        return jnp.concatenate([part[pl.ds(a, rows), :] for a in at], axis=0)

    each = nplane // PIECES
    swaps = []
    for q in range(PIECES):
        for n in range(q * each, (q + 1) * each):
            pair_out[n] = share(plane_peer(PLANE[n])[0], 1 - core).astype(pair_out.dtype)
        swap = pltpu.make_async_remote_copy(
            src_ref=pair_out.at[pl.ds(q * each, each)], dst_ref=pair_in.at[pl.ds(q * each, each)],
            send_sem=s0.at[q], recv_sem=r0.at[q], device_id=pair, device_id_type=MESH,
        )
        swap.start()
        swaps.append(swap)

    hear(1)
    tell(2)
    sent = []
    acc = None
    for q in range(PIECES):
        swaps[q].wait_recv()
        for n in range(q * each, (q + 1) * each):
            j, peer = plane_peer(PLANE[n])
            both = share(j, core) + pair_in[n].astype(jnp.float32)
            if n == nplane - 1:
                acc = both
                continue
            plane_out[n] = both.astype(plane_out.dtype)
            copy = pltpu.make_async_remote_copy(
                src_ref=plane_out.at[n], dst_ref=plane_in.at[n], send_sem=s1.at[n], recv_sem=r1.at[n],
                device_id=peer, device_id_type=MESH,
            )
            copy.start()
            sent.append(copy)
    for n in reversed(range(nplane - 1)):
        sent[n].wait_recv()
        acc += plane_in[n].astype(jnp.float32)

    for h in range(NZH):
        for q in range(nc):
            line_out[h * nc + q] = acc[h * rows:(h + 1) * rows, q * wide:(q + 1) * wide]
    hear(2)
    last = []
    for n, k in enumerate(line_steps):
        j, peer = line_peer(k)
        copy = pltpu.make_async_remote_copy(
            src_ref=line_out.at[j], dst_ref=line_in.at[n], send_sem=s2.at[n], recv_sem=r2.at[n],
            device_id=peer, device_id_type=MESH,
        )
        copy.start()
        last.append(copy)
    total = line_out[z]
    for n in reversed(range(nline - 1)):
        last[n].wait_recv()
        total += line_in[n]
    total_ref[...] = total
    for copy in [up, down] + swaps + sent + last:
        copy.wait_send()


def finish(scale, image_ref, total_ref, image_out, projected_out, scaled, sem):
    size = image_ref.shape[0] // WRITES
    writes = [
        pltpu.make_async_copy(
            image_ref.at[pl.ds(q * size, size)], image_out.at[pl.ds(q * size, size)], sem.at[q]
        )
        for q in range(WRITES)
    ]
    for write in writes:
        write.start()
    scaled[...] = total_ref[...] * scale
    small = pltpu.make_async_copy(scaled, projected_out, sem.at[WRITES])
    small.start()
    for write in writes + [small]:
        write.wait()


def local(basis, jac_blocks, block_cols, live_slots, accumulation):
    nrows, width = basis.shape
    nblk, slots, bs, _ = jac_blocks.shape
    mesh_count, col_count = lax.axis_size("mesh"), lax.axis_size("col")
    rows, wide = width // mesh_count, width // col_count
    nplane, nline = NX * NY, NZH * col_count
    span = (GROUP + 2 * REACH) * bs
    ngroup = nblk // GROUP
    lanes = 2 * bs
    image, total = pl.pallas_call(
        kernel,
        out_shape=(
            pltpu.VMEM((nrows, width), jnp.bfloat16),
            pltpu.VMEM((rows, wide), jnp.float32),
        ),
        in_specs=[pl.BlockSpec(memory_space=pl.ANY)] * 5,
        out_specs=(pl.BlockSpec(memory_space=pltpu.VMEM), pl.BlockSpec(memory_space=pltpu.VMEM)),
        scratch_shapes=[
            pltpu.VMEM((nrows + 2 * REACH * bs, width), jnp.bfloat16),
            pltpu.VMEM((nblk, slots, bs, bs), jnp.bfloat16),
            pltpu.SMEM((slots, nblk), jnp.int32),
            pltpu.SMEM((nblk,), jnp.int32),
            pltpu.VMEM((nrows // lanes, lanes), jnp.float32),
            pltpu.VMEM((ngroup, GROUP * bs, span), jnp.bfloat16),
            pltpu.VMEM((ngroup, GROUP * bs, span), jnp.bfloat16),
            pltpu.VMEM((width, width), jnp.float32),
            pltpu.VMEM((nplane, NZH * rows, width), jnp.bfloat16),
            pltpu.VMEM((nplane, NZH * rows, width), jnp.bfloat16),
            pltpu.VMEM((nplane - 1, NZH * rows, width), jnp.bfloat16),
            pltpu.VMEM((nplane - 1, NZH * rows, width), jnp.bfloat16),
            pltpu.VMEM((nline, rows, wide), jnp.float32),
            pltpu.VMEM((nline - 1, rows, wide), jnp.float32),
            pltpu.SemaphoreType.DMA((3,)),
            pltpu.SemaphoreType.DMA((ngroup,)),
            pltpu.SemaphoreType.DMA((ngroup,)),
            pltpu.SemaphoreType.DMA((2,)),
            pltpu.SemaphoreType.DMA((2,)),
            pltpu.SemaphoreType.REGULAR((len(FAR),)),
            pltpu.SemaphoreType.DMA((PIECES,)),
            pltpu.SemaphoreType.DMA((PIECES,)),
            pltpu.SemaphoreType.DMA((nplane - 1,)),
            pltpu.SemaphoreType.DMA((nplane - 1,)),
            pltpu.SemaphoreType.DMA((nline - 1,)),
            pltpu.SemaphoreType.DMA((nline - 1,)),
        ],
        compiler_params=pltpu.CompilerParams(
            collective_id=0, has_side_effects=True, vmem_limit_bytes=56 << 20
        ),
    )(basis, jac_blocks, block_cols.T, live_slots, accumulation.reshape(nrows // lanes, lanes))
    image = pltpu.with_memory_space_constraint(image, pltpu.VMEM)
    total = pltpu.with_memory_space_constraint(total, pltpu.VMEM)
    return pl.pallas_call(
        functools.partial(finish, 1.0 / (nrows * mesh_count * col_count)),
        out_shape=(
            jax.ShapeDtypeStruct((nrows, width), jnp.bfloat16),
            jax.ShapeDtypeStruct((rows, wide), jnp.float32),
        ),
        in_specs=[pl.BlockSpec(memory_space=pltpu.VMEM)] * 2,
        out_specs=(pl.BlockSpec(memory_space=pl.ANY), pl.BlockSpec(memory_space=pl.ANY)),
        scratch_shapes=[pltpu.VMEM((rows, wide), jnp.float32), pltpu.SemaphoreType.DMA((WRITES + 1,))],
    )(image, total)


def solution(mesh):
    return jax.shard_map(
        local,
        mesh=mesh,
        in_specs=(
            P(("mesh", "col"), None),
            P(("mesh", "col"), None, None, None),
            P(("mesh", "col"), None),
            P(("mesh", "col")),
            P(("mesh", "col")),
        ),
        out_specs=(P(("mesh", "col"), None), P("mesh", "col")),
        check_vma=False,
    )
```

```python
import functools

import jax
import jax.numpy as jnp
from jax import lax
from jax.experimental import pallas as pl
from jax.experimental.pallas import tpu as pltpu
from jax.sharding import PartitionSpec as P

REACH = 2
GROUP = 4
MESH = pl.DeviceIdType.MESH
NCORE, NX, NY, NZH = 2, 4, 4, 2
PIECES = 4
WRITES = 6
FAR = (1, 2, 4)


def hops(step, size):
    return min(step, size - step)


PLANE = sorted(
    ((dx, dy) for dx in range(NX) for dy in range(NY)), key=lambda d: -hops(d[0], NX) - hops(d[1], NY)
)


def kernel(
    basis_ref, jac_ref, cols_ref, live_ref, acc_ref, image_ref, total_ref,
    pad, jac, cols, live, gain, top, rest, part, pair_out, pair_in, plane_out, plane_in, line_out, line_in,
    local_sem, jac_sem, basis_sem, halo_send, halo_recv, known, s0, r0, s1, r1, s2, r2,
):
    m, c = lax.axis_index("mesh"), lax.axis_index("col")
    nm, nc = lax.axis_size("mesh"), lax.axis_size("col")
    core = m % NCORE
    x = (m // NCORE) % NX
    y = (m // (NCORE * NX)) % NY
    zh = m // (NCORE * NX * NY)
    z = zh * nc + c
    nplane, nline = NX * NY, NZH * nc
    line_steps = sorted(range(1, nline), key=lambda k: -hops(k, nline))

    nblk, slots, bs, _ = jac.shape
    nrows, width = basis_ref.shape
    reach = REACH * bs
    span = GROUP * bs + 2 * reach
    lanes = 2 * bs
    step = GROUP * bs
    ngroup = nblk // GROUP
    rows = total_ref.shape[0]
    wide = total_ref.shape[1]

    def plane_peer(step):
        px, py = (x + step[0]) % NX, (y + step[1]) % NY
        return py * NX + px, (((zh * NY + py) * NX + px) * NCORE + core, c)

    def line_peer(k):
        pz = (z + k) % nline
        return pz, ((pz // nc) * (NCORE * NX * NY) + m % (NCORE * NX * NY), pz % nc)

    index = m * nc + c
    before, after = (index + nm * nc - 1) % (nm * nc), (index + 1) % (nm * nc)
    low_peer, high_peer = (before // nc, before % nc), (after // nc, after % nc)
    pair = (m + 1 - 2 * core, c)

    moves = [
        pltpu.make_async_copy(cols_ref, cols, local_sem.at[0]),
        pltpu.make_async_copy(live_ref, live, local_sem.at[1]),
        pltpu.make_async_copy(acc_ref, gain, local_sem.at[2]),
    ]

    def jac_move(g):
        part_of = pl.ds(g * GROUP, GROUP)
        return pltpu.make_async_copy(jac_ref.at[part_of], jac.at[part_of], jac_sem.at[g])

    def basis_move(g):
        return pltpu.make_async_copy(
            basis_ref.at[pl.ds(g * step, step)], pad.at[pl.ds(reach + g * step, step)], basis_sem.at[g]
        )

    for move in moves:
        move.start()
    inner = ngroup - 2
    jac_move(1).start()
    for g in range(ngroup):
        basis_move(g).start()
    for g in [*range(2, ngroup - 1), 0, ngroup - 1]:
        jac_move(g).start()

    barrier = pltpu.get_barrier_semaphore()
    beside = [line_peer(1)[1], line_peer(nline - 1)[1]]
    peers = [low_peer, high_peer] + beside + [plane_peer(step)[1] for step in PLANE[:-1]] + [pair]
    for peer in peers:
        pl.semaphore_signal(barrier, inc=1, device_id=peer, device_id_type=MESH)

    for move in moves:
        move.wait()

    first = index * nblk
    left = lax.broadcasted_iota(jnp.int32, (1, lanes), 1) < bs
    lane = lax.broadcasted_iota(jnp.int32, (bs, lanes), 1)
    row = lax.broadcasted_iota(jnp.int32, (bs, lanes), 0)

    def build(g):
        for i in range(GROUP):
            r = g * GROUP + i
            own = first + r
            place = [jnp.where(s < live[r], cols[s, r] - own + REACH, -slots) for s in range(slots)]
            tiles = [jnp.zeros((bs, lanes), jnp.float32) for _ in range(3)]
            for p in range(0, slots, 2):
                a, b = jac[r, p], jac[r, p + 1]
                straight = jnp.concatenate([a, b], axis=1).astype(jnp.float32)
                crossed = jnp.concatenate([b, a], axis=1).astype(jnp.float32)
                where_s = jnp.where(left, place[p], place[p + 1])
                where_c = jnp.where(left, place[p + 1], place[p])
                for t in range(3):
                    w = 2 * (t + i // 2) - i
                    goal = jnp.where(left, w, w + 1)
                    tiles[t] += straight * (where_s == goal).astype(jnp.float32)
                    tiles[t] += crossed * (where_c == goal).astype(jnp.float32)
            t = (i + REACH) // 2 - i // 2
            gains = gain[pl.ds(g * (GROUP // 2) + i // 2, 1), :]
            tiles[t] += jnp.where(lane == row + bs * (i % 2), gains, 0.0)
            for t in range(span // lanes):
                k = t - i // 2
                here = (g, pl.ds(i * bs, bs), pl.ds(t * lanes, lanes))
                if 0 <= k < 3:
                    big = tiles[k].astype(jnp.bfloat16)
                    top[here] = big
                    rest[here] = (tiles[k] - big.astype(jnp.float32)).astype(jnp.bfloat16)
                else:
                    top[here] = jnp.zeros((bs, lanes), jnp.bfloat16)
                    rest[here] = jnp.zeros((bs, lanes), jnp.bfloat16)

    jac_move(1).wait()
    build(1)
    for g in range(ngroup):
        basis_move(g).wait()
    part[...] = jnp.zeros_like(part)

    up = pltpu.make_async_remote_copy(
        src_ref=pad.at[pl.ds(nrows, reach)], dst_ref=pad.at[pl.ds(0, reach)],
        send_sem=halo_send.at[0], recv_sem=halo_recv.at[0], device_id=high_peer, device_id_type=MESH,
    )
    down = pltpu.make_async_remote_copy(
        src_ref=pad.at[pl.ds(reach, reach)], dst_ref=pad.at[pl.ds(reach + nrows, reach)],
        send_sem=halo_send.at[1], recv_sem=halo_recv.at[1], device_id=low_peer, device_id_type=MESH,
    )
    meet_at = inner * jnp.where((z == 0) | (z == nline - 1), 1, 0)

    def tell(k):
        for peer in (line_peer(FAR[k])[1], line_peer(nline - FAR[k])[1]):
            pl.semaphore_signal(known.at[k], inc=1, device_id=peer, device_id_type=MESH)

    def hear(k):
        pl.semaphore_wait(known.at[k], 2)

    far_low = jnp.where(c == 0, 1, 0)

    def ends(k):
        return jnp.where(k == inner + far_low, 1, 0), jnp.where(k == inner + 1 - far_low, 1, 0)

    def order(k):
        low_now, high_now = ends(k)
        return (1 - low_now - high_now) * (k + 1) + high_now * (ngroup - 1)

    def ready(k):
        low_now, high_now = ends(k)

        @pl.when(k == meet_at)
        def _():
            pl.semaphore_wait(barrier, len(peers))
            @pl.when(far_low == 1)
            def _():
                down.start()
                up.start()

            @pl.when(far_low == 0)
            def _():
                up.start()
                down.start()

            tell(0)

        @pl.when(low_now == 1)
        def _():
            up.wait_recv()

        @pl.when(high_now == 1)
        def _():
            down.wait_recv()

    def multiply(g):
        at = pl.multiple_of(g * step, step)
        window = pad[pl.ds(at, span), :]
        out = jnp.dot(top[g], window, preferred_element_type=jnp.float32)
        out += jnp.dot(rest[g], window, preferred_element_type=jnp.float32)
        out = out.astype(image_ref.dtype)
        image_ref[pl.ds(at, step), :] = out
        part[...] += lax.dot_general(
            pad[pl.ds(reach + at, step), :], out, (((0,), (0,)), ((), ())), preferred_element_type=jnp.float32
        )

    def both(k, carry):
        ready(k)
        later = order(k + 1)
        jac_move(later).wait()
        multiply(order(k))
        build(later)
        return carry

    lax.fori_loop(0, ngroup - 1, both, 0)
    hear(0)
    tell(1)
    ready(ngroup - 1)
    multiply(order(ngroup - 1))

    def share(j, which):
        at = [pl.multiple_of(((h * nplane + j) * NCORE + which) * rows, rows) for h in range(NZH)]
        return jnp.concatenate([part[pl.ds(a, rows), :] for a in at], axis=0)

    each = nplane // PIECES
    swaps = []
    for q in range(PIECES):
        for n in range(q * each, (q + 1) * each):
            pair_out[n] = share(plane_peer(PLANE[n])[0], 1 - core).astype(pair_out.dtype)
        swap = pltpu.make_async_remote_copy(
            src_ref=pair_out.at[pl.ds(q * each, each)], dst_ref=pair_in.at[pl.ds(q * each, each)],
            send_sem=s0.at[q], recv_sem=r0.at[q], device_id=pair, device_id_type=MESH,
        )
        swap.start()
        swaps.append(swap)

    sent = []
    acc = None
    for q in range(PIECES):
        swaps[q].wait_recv()
        for n in range(q * each, (q + 1) * each):
            j, peer = plane_peer(PLANE[n])
            both = share(j, core) + pair_in[n].astype(jnp.float32)
            if n == nplane - 1:
                acc = both
                continue
            plane_out[n] = both.astype(plane_out.dtype)
            copy = pltpu.make_async_remote_copy(
                src_ref=plane_out.at[n], dst_ref=plane_in.at[n], send_sem=s1.at[n], recv_sem=r1.at[n],
                device_id=peer, device_id_type=MESH,
            )
            copy.start()
            sent.append(copy)
    hear(1)
    tell(2)
    for n in reversed(range(nplane - 1)):
        sent[n].wait_recv()
        acc += plane_in[n].astype(jnp.float32)

    for h in range(NZH):
        for q in range(nc):
            line_out[h * nc + q] = acc[h * rows:(h + 1) * rows, q * wide:(q + 1) * wide]
    hear(2)
    last = []
    for n, k in enumerate(line_steps):
        j, peer = line_peer(k)
        copy = pltpu.make_async_remote_copy(
            src_ref=line_out.at[j], dst_ref=line_in.at[n], send_sem=s2.at[n], recv_sem=r2.at[n],
            device_id=peer, device_id_type=MESH,
        )
        copy.start()
        last.append(copy)
    total = line_out[z]
    for n in reversed(range(nline - 1)):
        last[n].wait_recv()
        total += line_in[n]
    total_ref[...] = total
    for copy in [up, down] + swaps + sent + last:
        copy.wait_send()


def finish(scale, image_ref, total_ref, image_out, projected_out, scaled, sem):
    size = image_ref.shape[0] // WRITES
    writes = [
        pltpu.make_async_copy(
            image_ref.at[pl.ds(q * size, size)], image_out.at[pl.ds(q * size, size)], sem.at[q]
        )
        for q in range(WRITES)
    ]
    for write in writes:
        write.start()
    scaled[...] = total_ref[...] * scale
    small = pltpu.make_async_copy(scaled, projected_out, sem.at[WRITES])
    small.start()
    for write in writes + [small]:
        write.wait()


def local(basis, jac_blocks, block_cols, live_slots, accumulation):
    nrows, width = basis.shape
    nblk, slots, bs, _ = jac_blocks.shape
    mesh_count, col_count = lax.axis_size("mesh"), lax.axis_size("col")
    rows, wide = width // mesh_count, width // col_count
    nplane, nline = NX * NY, NZH * col_count
    span = (GROUP + 2 * REACH) * bs
    ngroup = nblk // GROUP
    lanes = 2 * bs
    image, total = pl.pallas_call(
        kernel,
        out_shape=(
            pltpu.VMEM((nrows, width), jnp.bfloat16),
            pltpu.VMEM((rows, wide), jnp.float32),
        ),
        in_specs=[pl.BlockSpec(memory_space=pl.ANY)] * 5,
        out_specs=(pl.BlockSpec(memory_space=pltpu.VMEM), pl.BlockSpec(memory_space=pltpu.VMEM)),
        scratch_shapes=[
            pltpu.VMEM((nrows + 2 * REACH * bs, width), jnp.bfloat16),
            pltpu.VMEM((nblk, slots, bs, bs), jnp.bfloat16),
            pltpu.SMEM((slots, nblk), jnp.int32),
            pltpu.SMEM((nblk,), jnp.int32),
            pltpu.VMEM((nrows // lanes, lanes), jnp.float32),
            pltpu.VMEM((ngroup, GROUP * bs, span), jnp.bfloat16),
            pltpu.VMEM((ngroup, GROUP * bs, span), jnp.bfloat16),
            pltpu.VMEM((width, width), jnp.float32),
            pltpu.VMEM((nplane, NZH * rows, width), jnp.bfloat16),
            pltpu.VMEM((nplane, NZH * rows, width), jnp.bfloat16),
            pltpu.VMEM((nplane - 1, NZH * rows, width), jnp.bfloat16),
            pltpu.VMEM((nplane - 1, NZH * rows, width), jnp.bfloat16),
            pltpu.VMEM((nline, rows, wide), jnp.float32),
            pltpu.VMEM((nline - 1, rows, wide), jnp.float32),
            pltpu.SemaphoreType.DMA((3,)),
            pltpu.SemaphoreType.DMA((ngroup,)),
            pltpu.SemaphoreType.DMA((ngroup,)),
            pltpu.SemaphoreType.DMA((2,)),
            pltpu.SemaphoreType.DMA((2,)),
            pltpu.SemaphoreType.REGULAR((len(FAR),)),
            pltpu.SemaphoreType.DMA((PIECES,)),
            pltpu.SemaphoreType.DMA((PIECES,)),
            pltpu.SemaphoreType.DMA((nplane - 1,)),
            pltpu.SemaphoreType.DMA((nplane - 1,)),
            pltpu.SemaphoreType.DMA((nline - 1,)),
            pltpu.SemaphoreType.DMA((nline - 1,)),
        ],
        compiler_params=pltpu.CompilerParams(
            collective_id=0, has_side_effects=True, vmem_limit_bytes=56 << 20
        ),
    )(basis, jac_blocks, block_cols.T, live_slots, accumulation.reshape(nrows // lanes, lanes))
    image = pltpu.with_memory_space_constraint(image, pltpu.VMEM)
    total = pltpu.with_memory_space_constraint(total, pltpu.VMEM)
    return pl.pallas_call(
        functools.partial(finish, 1.0 / (nrows * mesh_count * col_count)),
        out_shape=(
            jax.ShapeDtypeStruct((nrows, width), jnp.bfloat16),
            jax.ShapeDtypeStruct((rows, wide), jnp.float32),
        ),
        in_specs=[pl.BlockSpec(memory_space=pltpu.VMEM)] * 2,
        out_specs=(pl.BlockSpec(memory_space=pl.ANY), pl.BlockSpec(memory_space=pl.ANY)),
        scratch_shapes=[pltpu.VMEM((rows, wide), jnp.float32), pltpu.SemaphoreType.DMA((WRITES + 1,))],
    )(image, total)


def solution(mesh):
    return jax.shard_map(
        local,
        mesh=mesh,
        in_specs=(
            P(("mesh", "col"), None),
            P(("mesh", "col"), None, None, None),
            P(("mesh", "col"), None),
            P(("mesh", "col")),
            P(("mesh", "col")),
        ),
        out_specs=(P(("mesh", "col"), None), P("mesh", "col")),
        check_vma=False,
    )
```
